32 devices in a mesh: grp: 2 (over y), inp: 8 (over z, x), freq: 2 (over core).
Axes of the slice: x: 2, y: 2, z: 4, core: 2. Of those that a mesh axis runs over, the one named last changes fastest.
Arguments:
- voltages: int32 [2048, 64, 2048], P(('grp', 'inp'), 'freq'), parts along dimension 0, may hold values from -127 to 127, as said below
- coeffs: int32 [8, 2048], replicated, may hold values from -6144 to 6144, as said below
Outputs:
- visibilities: bfloat16 [1024, 2, 36, 128, 128], P(('grp', 'inp', 'freq')), parts along dimension 0
The draws below stay inside these ranges and needn't reach their ends.
There are 2 independent parts, one for each index of `grp`. The reference program is written for one: setup_inputs(seed, part) draws one part's arguments, and reference() takes and returns one part's arrays. A program takes and returns all parts, laid end to end along the dimension named above; an argument that names none is the same for every part. Nothing has to cross between parts.
Inputs may be any that keep to these rules, and one draw needn't show every extreme that they name: `voltages`: signed 8-bit samples. `coeffs`: integer coefficients.
All inputs are finite; a program needn't handle non-finite values.
Results may differ from the reference program's by a relative error of at most 0.0069.
Values may be sent and summed in bfloat16 or wider, within the bound.
A program may use at most 384 MiB of HBM per device.

```python
import math
import jax
import jax.numpy as jnp
from jax import lax

SPF = 2048
TAPS = 8
CH = 512
CH0 = 256
INPUTS = 1024
BLK = 128
NBLK = 8
FRAMES = 64


def draw_voltages(key, part):
    key_base, key_values = jax.random.split(jax.random.fold_in(key, 11))
    base = jax.random.randint(key_base, (INPUTS, 1, 1), 4, 32)
    frame = jnp.arange(FRAMES, dtype=jnp.int32)[None, :, None]
    limit = base * (FRAMES + 3 * frame) // FRAMES
    limit = jnp.broadcast_to(limit, (INPUTS, FRAMES, SPF))
    return jax.random.randint(key_values, (INPUTS, FRAMES, SPF), -limit, limit + 1).astype(jnp.int32)


def draw_coeffs(key, part):
    length = TAPS * SPF
    place = jnp.arange(length, dtype=jnp.int32)
    tent = jnp.minimum(place + 1, length - place) * 8192 // length
    tap = place // SPF
    sign = 1 - 2 * (jnp.abs(2 * tap - (TAPS - 1)) // 2 % 2)
    noise = jax.random.randint(jax.random.fold_in(key, 23), (length,), -(tent // 2), tent // 2 + 1)
    return (sign * tent + noise).reshape(TAPS, SPF).astype(jnp.int32)


def setup_inputs(seed: int = 0, part: int = 0) -> dict:
    streams_of = jax.random.split(jax.random.key(seed), 3)
    own_keys = jax.random.split(jax.random.fold_in(streams_of[2], part), 3)
    voltages = draw_voltages(jax.random.fold_in(jax.random.fold_in(streams_of[2], part), 71), part)
    coeffs = draw_coeffs(jax.random.fold_in(streams_of[2], 71), part)
    return dict(voltages=voltages, coeffs=coeffs)


def make_table():
    sample = jnp.arange(SPF, dtype=jnp.int32)[:, None]
    channel = jnp.arange(CH, dtype=jnp.int32)[None, :] + CH0
    phase = sample * channel % SPF
    angle = phase.astype(jnp.float32) * (2.0 * math.pi / SPF)
    return jnp.concatenate([jnp.cos(angle), -jnp.sin(angle)], axis=1).astype(jnp.bfloat16)

def block_pairs():
    return [(row_index, col_index) for row_index in range(NBLK) for col_index in range(row_index, NBLK)]

def reference(voltages, coeffs):
    dft_table = make_table().astype(jnp.float32)
    weights = coeffs.astype(jnp.float32)

    def front_end(samples):
        padded = jnp.pad(samples.astype(jnp.float32), ((0, 0), (TAPS - 1, 0), (0, 0)))
        summed = jnp.zeros((samples.shape[0], FRAMES, SPF), jnp.float32)
        for tap_index in range(TAPS):
            begin = TAPS - 1 - tap_index
            summed = summed + weights[tap_index] * padded[:, begin:begin + FRAMES, :]
        rounded = lax.optimization_barrier(summed.astype(jnp.bfloat16))
        filtered = rounded.astype(jnp.float32)
        spectrum = jnp.dot(filtered.reshape(-1, SPF), dft_table, precision=lax.Precision.HIGHEST, preferred_element_type=jnp.float32).reshape(-1, FRAMES, 2 * CH)
        power = lax.optimization_barrier(jnp.sum(spectrum * spectrum, axis=(1, 2))) / (FRAMES * CH)
        gains = 1.0 / jnp.sqrt(power + 1e-06)
        return (spectrum * gains[:, None, None]).astype(jnp.bfloat16)
    blocked = voltages.reshape(NBLK, BLK, FRAMES, SPF)
    scaled = lax.map(front_end, blocked).reshape(INPUTS, FRAMES, 2, CH)
    stacked = jnp.transpose(scaled, (3, 0, 2, 1)).reshape(CH, INPUTS, 2 * FRAMES)
    pairs = block_pairs()

    def correlate(operand):
        first = operand.astype(jnp.float32)
        second = jnp.concatenate([-first[:, FRAMES:], first[:, :FRAMES]], axis=1)
        real_part = jnp.dot(first, first.T, precision=lax.Precision.HIGHEST, preferred_element_type=jnp.float32)
        imag_part = jnp.dot(first, second.T, precision=lax.Precision.HIGHEST, preferred_element_type=jnp.float32)
        grams = jnp.stack([real_part, imag_part]) * (1.0 / FRAMES)
        picked = jnp.stack([grams[:, row_index * BLK:(row_index + 1) * BLK, col_index * BLK:(col_index + 1) * BLK] for row_index, col_index in pairs], axis=1)
        return picked.astype(jnp.bfloat16)
    return lax.map(correlate, stacked)
```

```python
import functools
import math

import jax
import jax.numpy as jnp
import numpy as np
from jax import lax
from jax.experimental import pallas as pl
from jax.experimental.pallas import tpu as pltpu
from jax.sharding import PartitionSpec as P

SPF = 2048
TAPS = 8
CH = 512
CH0 = 256
INPUTS = 1024
BLK = 128


def passed_along(x, axis, by):
    length = lax.axis_size(axis)
    pairs = [(i, i + by) for i in range(length) if 0 <= i + by < length]
    return lax.ppermute(x, axis, pairs)


def make_table():
    sample = jnp.arange(SPF, dtype=jnp.int32)[:, None]
    channel = jnp.arange(CH, dtype=jnp.int32)[None, :] + CH0
    phase = sample * channel % SPF
    angle = phase.astype(jnp.float32) * (2.0 * math.pi / SPF)
    return jnp.concatenate([jnp.cos(angle), -jnp.sin(angle)], axis=1).astype(jnp.bfloat16)


def plain_device(voltages, coeffs):
    inputs_here = voltages.shape[0]
    frames_here = voltages.shape[1]
    inp_count = lax.axis_size("inp")
    freq_count = lax.axis_size("freq")
    frames_all = frames_here * freq_count
    history = voltages[:, frames_here - (TAPS - 1) :, :].astype(jnp.bfloat16)
    earlier = passed_along(history, "freq", 1)
    extended = jnp.concatenate([earlier.astype(jnp.float32), voltages.astype(jnp.float32)], axis=1)
    weights = coeffs.astype(jnp.float32)
    summed = jnp.zeros((inputs_here, frames_here, SPF), jnp.float32)
    for tap_index in range(TAPS):
        begin = TAPS - 1 - tap_index
        summed = summed + weights[tap_index] * extended[:, begin : begin + frames_here, :]
    filtered = summed.astype(jnp.bfloat16).reshape(inputs_here * frames_here, SPF)
    spectrum_t = jnp.einsum("nj,rn->jr", make_table(), filtered, preferred_element_type=jnp.float32)
    spectrum_t = spectrum_t.reshape(2 * CH, inputs_here, frames_here)
    squares = jnp.sum(spectrum_t * spectrum_t, axis=(0, 2))
    power = lax.psum(squares, "freq") / (frames_all * CH)
    gains = 1.0 / jnp.sqrt(power + 1e-06)
    scaled = (spectrum_t * gains[None, :, None]).astype(jnp.bfloat16)
    scaled = scaled.reshape(2, CH, inputs_here * frames_here)
    arrived = lax.all_to_all(scaled[None], ("inp", "freq"), split_axis=2, concat_axis=0, tiled=True)
    width_here = arrived.shape[-2]
    arranged = arrived.reshape(inp_count, freq_count, 2, width_here, inputs_here, frames_here)
    arranged = jnp.transpose(arranged, (3, 0, 4, 2, 1, 5))
    stacked = arranged.reshape(width_here, INPUTS, 2 * frames_all)
    other = jnp.concatenate([-stacked[:, :, frames_all:], stacked[:, :, :frames_all]], axis=2)
    block_count = INPUTS // BLK
    scale = 1.0 / frames_all
    pieces = []
    for row_index in range(block_count):
        row_panel = stacked[:, row_index * BLK : (row_index + 1) * BLK]
        real_part = jnp.einsum(
            "cut,cmt->cum",
            row_panel,
            stacked[:, row_index * BLK :],
            preferred_element_type=jnp.float32,
        )
        imag_part = jnp.einsum(
            "cut,cmt->cum",
            row_panel,
            other[:, row_index * BLK :],
            preferred_element_type=jnp.float32,
        )
        band = jnp.stack([real_part, imag_part], axis=1) * scale
        for col_index in range(row_index, block_count):
            begin = (col_index - row_index) * BLK
            pieces.append(band[:, :, :, begin : begin + BLK])
    return jnp.stack(pieces, axis=2).astype(jnp.bfloat16)


MESH = pl.DeviceIdType.MESH
STEP = 8
LANE = 128
PLANE = 4
PLANES = 4
LATE = 8
MOVES = 4
PAIR = 2


def table_rows(count):
    sample = np.arange(SPF, dtype=np.int32)[None, :]
    channel = np.arange(CH, dtype=np.int32)[:, None] + CH0
    angle = (sample * channel % SPF).astype(np.float32) * np.float32(2.0 * math.pi / SPF)
    both = np.stack([np.cos(angle), -np.sin(angle)])
    rows = both.reshape(2, count, CH // count, SPF).transpose(1, 0, 2, 3).reshape(2 * CH, SPF)
    return jnp.asarray(rows.astype(jnp.bfloat16))


def moved(index, move):
    plane, spot = index // PLANE, index % PLANE
    plane = (plane + PLANES // 2) % PLANES if move < 2 else PLANES - 1 - plane
    spot = spot if move % 2 == 0 else spot + 1 - 2 * (spot % 2)
    return plane * PLANE + spot


def trades_late(one, other):
    across = (one // (PLANE * 2)) != (other // (PLANE * 2))
    return across & ((one % PLANE) // 2 == (other % PLANE) // 2)


def front_kernel(inp_count, freq_count, late, *refs):
    volts, coeffs, table_hbm, spec, arrived, powers = refs[:6]
    moves = MOVES if late else 0
    lates = refs[6 : 6 + moves]
    (
        frames,
        weights,
        table,
        filtered,
        spread,
        staged,
        power,
        load_sem,
        table_sem,
        hist_send,
        hist_recv,
        stage_sem,
        send_sem,
        recv_sem,
        pow_sem,
        pow_send,
        pow_recv,
    ) = refs[6 + moves :]
    grp = lax.axis_index("grp")
    inp = lax.axis_index("inp")
    freq = lax.axis_index("freq")
    count = inp_count * freq_count
    me = inp * freq_count + freq
    inputs_here, frames_here, _ = volts.shape
    blocks = frames_here // STEP
    taps = coeffs.shape[0]
    past = taps - 1
    width = staged.shape[2]
    soon = width - late
    rows = PLANE * 2 * width
    half = SPF // 2

    def where(index):
        return (grp, index // freq_count, index % freq_count)

    def load(t, side):
        return pltpu.make_async_copy(
            volts.at[:, t, pl.ds(side * half, half)],
            frames.at[t + past, :, pl.ds(side * half, half)],
            load_sem.at[side, t],
        )

    table_copy = pltpu.make_async_copy(table_hbm, table, table_sem)
    for side in range(2):
        for t in range(frames_here - STEP - past, frames_here):
            load(t, side).start()
        if side == 0:
            table_copy.start()
    for t in reversed(range(frames_here - STEP - past)):
        for side in range(2):
            load(t, side).start()

    barrier = pltpu.get_barrier_semaphore()

    def greet(step, carry):
        other = (me + step) % count
        pl.semaphore_signal(barrier, inc=1, device_id=where(other), device_id_type=MESH)
        return carry

    lax.fori_loop(1, count, greet, 0)
    power[...] = jnp.zeros_like(power)
    weights[...] = coeffs[...].astype(jnp.float32)

    @pl.when(freq == 0)
    def _():
        def clear(step, carry):
            frames[step] = jnp.zeros((inputs_here, SPF), jnp.int32)
            return carry

        lax.fori_loop(0, past, clear, 0)

    def history_copy(step):
        return pltpu.make_async_remote_copy(
            src_ref=volts.at[:, frames_here - past + step, :],
            dst_ref=frames.at[step],
            send_sem=hist_send.at[step],
            recv_sem=hist_recv.at[step],
            device_id=(grp, inp, 1),
            device_id_type=MESH,
        )

    def filter_side(first, side):
        lanes = half // LANE

        def tile(index, carry):
            row = pl.multiple_of(index // lanes * 16, 16)
            col = pl.multiple_of(side * half + index % lanes * LANE, LANE)
            window = [
                frames[first + k, pl.ds(row, 16), pl.ds(col, LANE)].astype(jnp.float32)
                for k in range(STEP + past)
            ]
            scales = [
                jnp.broadcast_to(weights[k : k + 1, pl.ds(col, LANE)], (16, LANE)) for k in range(taps)
            ]
            for t in range(STEP):
                total = scales[0] * window[past + t]
                for k in range(1, taps):
                    total = total + scales[k] * window[past + t - k]
                at = pl.multiple_of(t * inputs_here + row, 16)
                filtered[pl.ds(at, 16), pl.ds(col, LANE)] = total.astype(jnp.bfloat16)
            return carry

        lax.fori_loop(0, inputs_here // 16 * lanes, tile, 0, unroll=4)

    def remote(block, other, part):
        return pltpu.make_async_remote_copy(
            src_ref=spec.at[other, block, :, pl.ds(0, part)],
            dst_ref=arrived.at[me, block, :, pl.ds(0, part)],
            send_sem=send_sem.at[block, other],
            recv_sem=recv_sem.at[block, me],
            device_id=where(other),
            device_id_type=MESH,
        )

    def landing(block, other, part):
        return pltpu.make_async_remote_copy(
            src_ref=spec.at[other, block, :, pl.ds(0, part)],
            dst_ref=arrived.at[other, block, :, pl.ds(0, part)],
            send_sem=send_sem.at[block, other],
            recv_sem=recv_sem.at[block, other],
            device_id=where(other),
            device_id_type=MESH,
        )

    def either(other, act):
        if not late:
            act(width)
            return

        @pl.when(trades_late(me, other))
        def _():
            act(soon)

        @pl.when(jnp.logical_not(trades_late(me, other)))
        def _():
            act(width)

    here = me // PLANE
    outer = (here == 0) | (here == PLANES - 1)
    near = here + 1 - 2 * (here % 2)
    jump = (here + PLANES // 2) % PLANES
    mirror = PLANES - 1 - here
    first_plane = jnp.where(outer, near, jump)
    second_plane = jnp.where(outer, jump, mirror)
    third_plane = jnp.where(outer, mirror, near)
    frames_step = STEP // 2

    def do_plane(block, plane):
        def transform(step, carry):
            lines = table[pl.ds(pl.multiple_of(plane * rows, rows), rows), :]
            at = pl.multiple_of(step * (frames_step * inputs_here), frames_step * inputs_here)
            chunk = filtered[pl.ds(at, frames_step * inputs_here), :]
            product = lax.dot_general(
                lines, chunk, (((1,), (1,)), ((), ())), preferred_element_type=jnp.float32
            )
            total = jnp.zeros((8, LANE), jnp.float32)
            for t in range(frames_step):
                piece = product[:, t * LANE : (t + 1) * LANE]
                spread[pl.ds(step * frames_step + t, rows, stride=STEP), :] = piece
                total = total + jnp.sum((piece * piece).reshape(rows // 8, 8, LANE), axis=0)
            power[...] += total
            return carry

        lax.fori_loop(0, STEP // frames_step, transform, 0)

        def convert(step, carry):
            at = pl.multiple_of(step * (2 * width * STEP), 2 * width * STEP)
            lump = spread[pl.ds(at, 2 * width * STEP), :].astype(jnp.bfloat16)
            staged[step] = lump.reshape(2, width, STEP, LANE)
            return carry

        lax.fori_loop(0, PLANE, convert, 0)

        def put_away(spot, start):
            owner = plane * PLANE + spot
            here_copy = pltpu.make_async_copy(
                staged.at[spot], arrived.at[owner, block], stage_sem.at[0, spot]
            )

            @pl.when(owner == me)
            def _():
                if start:
                    here_copy.start()
                else:
                    here_copy.wait()

            @pl.when(owner != me)
            def _():
                def act(part):
                    away = pltpu.make_async_copy(
                        staged.at[spot, :, pl.ds(0, part)],
                        spec.at[owner, block, :, pl.ds(0, part)],
                        stage_sem.at[0, spot],
                    )
                    if start:
                        away.start()
                    else:
                        away.wait()
                        remote(block, owner, part).start()

                either(owner, act)

            for move in range(moves):

                @pl.when(owner == moved(me, move))
                def _():
                    keep = pltpu.make_async_copy(
                        staged.at[spot, :, pl.ds(soon, late)], lates[move].at[block], stage_sem.at[1, spot]
                    )
                    if start:
                        keep.start()
                    else:
                        keep.wait()

        for spot in range(PLANE):
            put_away(spot, True)
        for spot in range(PLANE):
            put_away(spot, False)

    def do_block(step, carry):
        block = blocks - 1 - step
        first = block * STEP
        start = jnp.maximum(first - past, 0)
        stop = jnp.where(step == 0, frames_here, first + STEP - past)

        @pl.when((block == 0) & (freq != 0))
        def _():
            for k in range(past):
                history_copy(k).wait_recv()

        def one_side(side, inner):
            def arrive(t, innermost):
                load(t, side).wait()
                return innermost

            lax.fori_loop(start, stop, arrive, 0)
            filter_side(first, side)
            return inner

        lax.fori_loop(0, 2, one_side, 0)

        @pl.when(step == 0)
        def _():
            table_copy.wait()
            pl.semaphore_wait(barrier, count - 1)

            @pl.when(freq == 0)
            def _():
                for k in range(past):
                    history_copy(k).start()

        def one_plane(turn, inner):
            plane = jnp.where(
                turn == 0,
                first_plane,
                jnp.where(turn == 1, second_plane, jnp.where(turn == 2, third_plane, here)),
            )
            do_plane(block, plane)
            return inner

        lax.fori_loop(0, PLANES, one_plane, 0)
        return carry

    lax.fori_loop(0, blocks, do_block, 0)

    power_copy = pltpu.make_async_copy(power, powers.at[me], pow_sem)
    power_copy.start()
    power_copy.wait()

    def power_remote(other):
        return pltpu.make_async_remote_copy(
            src_ref=powers.at[me],
            dst_ref=powers.at[me],
            send_sem=pow_send.at[other],
            recv_sem=pow_recv.at[me],
            device_id=where(other),
            device_id_type=MESH,
        )

    def send_power(step, carry):
        power_remote((me + step) % count).start()
        return carry

    lax.fori_loop(1, count, send_power, 0)

    @pl.when(freq == 0)
    def _():
        for step in range(past):
            history_copy(step).wait_send()

    def finish(step, carry):
        other = (me + step) % count

        def act(part):
            for block in range(blocks):
                remote(block, other, part).wait_send()
                landing(block, other, part).wait_recv()

        either(other, act)
        power_remote(other).wait_send()
        pltpu.make_async_remote_copy(
            src_ref=powers.at[other],
            dst_ref=powers.at[other],
            send_sem=pow_send.at[other],
            recv_sem=pow_recv.at[other],
            device_id=where(other),
            device_id_type=MESH,
        ).wait_recv()
        return carry

    lax.fori_loop(1, count, finish, 0)


def front(voltages, coeffs, inp_count, freq_count, late):
    inputs_here, frames_here, _ = voltages.shape
    taps = coeffs.shape[0]
    count = inp_count * freq_count
    width = CH // count
    blocks = frames_here // STEP
    moves = MOVES if late else 0
    anywhere = pl.BlockSpec(memory_space=pl.ANY)
    lumps = jax.ShapeDtypeStruct((count, blocks, 2, width, STEP, LANE), jnp.bfloat16)
    kept = jax.ShapeDtypeStruct((blocks, 2, late, STEP, LANE), jnp.bfloat16)
    return pl.pallas_call(
        functools.partial(front_kernel, inp_count, freq_count, late),
        out_shape=(lumps, lumps, jax.ShapeDtypeStruct((count, 8, LANE), jnp.float32)) + (kept,) * moves,
        in_specs=[anywhere, pl.BlockSpec(memory_space=pltpu.VMEM), anywhere],
        out_specs=(anywhere,) * (3 + moves),
        scratch_shapes=[
            pltpu.VMEM((frames_here + taps - 1, inputs_here, SPF), jnp.int32),
            pltpu.VMEM((taps, SPF), jnp.float32),
            pltpu.VMEM((2 * CH, SPF), jnp.bfloat16),
            pltpu.VMEM((STEP * inputs_here, SPF), jnp.bfloat16),
            pltpu.VMEM((PLANE * 2 * width * STEP, LANE), jnp.float32),
            pltpu.VMEM((PLANE, 2, width, STEP, LANE), jnp.bfloat16),
            pltpu.VMEM((8, LANE), jnp.float32),
            pltpu.SemaphoreType.DMA((2, frames_here)),
            pltpu.SemaphoreType.DMA,
            pltpu.SemaphoreType.DMA((taps - 1,)),
            pltpu.SemaphoreType.DMA((taps - 1,)),
            pltpu.SemaphoreType.DMA((2, PLANE)),
            pltpu.SemaphoreType.DMA((blocks, count)),
            pltpu.SemaphoreType.DMA((blocks, count)),
            pltpu.SemaphoreType.DMA,
            pltpu.SemaphoreType.DMA((count,)),
            pltpu.SemaphoreType.DMA((count,)),
        ],
        compiler_params=pltpu.CompilerParams(
            collective_id=0, has_side_effects=True, vmem_limit_bytes=67043328
        ),
        name="front",
    )(voltages, coeffs, table_rows(count))


def set_gains(powers, gain_row, gain_col, frames_all):
    panels = gain_row.shape[0]
    freq_count = powers.shape[0] // panels
    for panel in range(panels):
        both = powers[panel * freq_count]
        for extra in range(1, freq_count):
            both = both + powers[panel * freq_count + extra]
        power = jnp.sum(both, axis=0, keepdims=True) / (frames_all * CH)
        gain = 1.0 / jnp.sqrt(power + 1e-06)
        gain_row[panel : panel + 1, :] = gain
        wide = jnp.broadcast_to(gain * (1.0 / frames_all), (BLK, BLK))
        gain_col[panel * BLK : (panel + 1) * BLK, :] = wide.T


def correlate_channel(piece, panels, gain_row, gain_col, out, turned):
    straight, crossed = [], []
    for panel in range(panels):
        real, imag = piece(panel, 0), piece(panel, 1)
        both = jnp.concatenate([real, imag], axis=0)
        straight.append(both)
        crossed.append(jnp.concatenate([-imag, real], axis=0))
        turned[panel * BLK : (panel + 1) * BLK, :] = both.T
    for col in range(panels):
        sides = jnp.concatenate([straight[col], crossed[col]], axis=1)
        product = jnp.dot(turned[: (col + 1) * BLK, :], sides, preferred_element_type=jnp.float32)
        for row in range(col + 1):
            pair = row * panels - row * (row - 1) // 2 + col - row
            gain = gain_col[row * BLK : (row + 1) * BLK, :] * gain_row[col : col + 1, :]
            part = product[row * BLK : (row + 1) * BLK]
            out[0, pair] = (part[:, :BLK] * gain).astype(jnp.bfloat16)
            out[1, pair] = (part[:, BLK:] * gain).astype(jnp.bfloat16)


def soon_kernel(frames_all, block, powers, out, gain_row, gain_col, turned):
    panels, freq_count, blocks = block.shape[:3]

    @pl.when(pl.program_id(0) == 0)
    def _():
        set_gains(powers, gain_row, gain_col, frames_all)

    for c in range(PAIR):

        def piece(panel, side):
            parts = [block[panel, f, b, side, c] for f in range(freq_count) for b in range(blocks)]
            return jnp.concatenate(parts, axis=0)

        correlate_channel(piece, panels, gain_row, gain_col, out.at[c], turned.at[c])


def late_kernel(frames_all, freq_count, *refs):
    arrived, powers = refs[1:3]
    got = refs[3 : 3 + MOVES]
    out, held, gain_row, gain_col, turned, sem = refs[3 + MOVES :]
    count, blocks, _, late = held.shape[:4]
    panels = count // freq_count
    soon = arrived.shape[3] - late
    me = lax.axis_index("inp") * freq_count + lax.axis_index("freq")

    @pl.when(pl.program_id(0) == 0)
    def _():
        def fetch(source):
            return pltpu.make_async_copy(
                arrived.at[source, :, :, pl.ds(soon, late)], held.at[source], sem.at[source]
            )

        for source in range(count):

            @pl.when(jnp.logical_not(trades_late(me, source)))
            def _():
                fetch(source).start()

        for move in range(MOVES):
            source = moved(me, move)
            pltpu.make_async_copy(got[move], held.at[source], sem.at[source]).start()
        set_gains(powers, gain_row, gain_col, frames_all)
        for source in range(count):
            fetch(source).wait()

    for c in range(PAIR):
        at = pl.program_id(0) * PAIR + c

        def piece(panel, side):
            parts = [
                held[panel * freq_count + f, b, side, at] for f in range(freq_count) for b in range(blocks)
            ]
            return jnp.concatenate(parts, axis=0)

        correlate_channel(piece, panels, gain_row, gain_col, out.at[c], turned.at[c])


def correlate(arrived, powers, inp_count, freq_count, frames_all, late):
    count, blocks, _, width, _, _ = arrived.shape
    pairs = inp_count * (inp_count + 1) // 2
    steps = (width - late) // PAIR
    lumps = arrived.reshape(inp_count, freq_count, blocks, 2, width, STEP, LANE)
    return pl.pallas_call(
        functools.partial(soon_kernel, frames_all),
        grid=(steps,),
        out_shape=jax.ShapeDtypeStruct((width, 2, pairs, BLK, BLK), jnp.bfloat16),
        in_specs=[
            pl.BlockSpec(
                (inp_count, freq_count, blocks, 2, PAIR, STEP, LANE), lambda c: (0, 0, 0, 0, c, 0, 0)
            ),
            pl.BlockSpec((count, 8, LANE), lambda c: (0, 0, 0)),
        ],
        out_specs=pl.BlockSpec((PAIR, 2, pairs, BLK, BLK), lambda c: (c, 0, 0, 0, 0)),
        scratch_shapes=[
            pltpu.VMEM((inp_count, LANE), jnp.float32),
            pltpu.VMEM((inp_count * BLK, BLK), jnp.float32),
            pltpu.VMEM((PAIR, inp_count * BLK, 2 * frames_all), jnp.bfloat16),
        ],
        compiler_params=pltpu.CompilerParams(vmem_limit_bytes=48 * 1024 * 1024),
        cost_estimate=pl.CostEstimate(
            flops=steps * PAIR * pairs * BLK * BLK * 8 * frames_all,
            bytes_accessed=steps * PAIR * pairs * BLK * BLK * 4,
            transcendentals=0,
        ),
        name="correlate",
    )(lumps, powers)


def correlate_late(begun, arrived, powers, got, inp_count, freq_count, frames_all, late):
    count, blocks, _, width, _, _ = arrived.shape
    pairs = inp_count * (inp_count + 1) // 2
    steps, first = late // PAIR, (width - late) // PAIR
    anywhere = pl.BlockSpec(memory_space=pl.ANY)
    return pl.pallas_call(
        functools.partial(late_kernel, frames_all, freq_count),
        grid=(steps,),
        out_shape=jax.ShapeDtypeStruct(begun.shape, begun.dtype),
        in_specs=[anywhere, anywhere, pl.BlockSpec((count, 8, LANE), lambda c: (0, 0, 0))]
        + [anywhere] * MOVES,
        out_specs=pl.BlockSpec((PAIR, 2, pairs, BLK, BLK), lambda c: (first + c, 0, 0, 0, 0)),
        scratch_shapes=[
            pltpu.VMEM((count, blocks, 2, late, STEP, LANE), jnp.bfloat16),
            pltpu.VMEM((inp_count, LANE), jnp.float32),
            pltpu.VMEM((inp_count * BLK, BLK), jnp.float32),
            pltpu.VMEM((PAIR, inp_count * BLK, 2 * frames_all), jnp.bfloat16),
            pltpu.SemaphoreType.DMA((count,)),
        ],
        input_output_aliases={0: 0},
        compiler_params=pltpu.CompilerParams(vmem_limit_bytes=48 * 1024 * 1024),
        cost_estimate=pl.CostEstimate(
            flops=steps * PAIR * pairs * BLK * BLK * 8 * frames_all,
            bytes_accessed=steps * PAIR * pairs * BLK * BLK * 4,
            transcendentals=0,
        ),
        name="correlate_late",
    )(begun, arrived, powers, *got)


def per_device(voltages, coeffs):
    inputs_here, frames_here, _ = voltages.shape
    inp_count = lax.axis_size("inp")
    freq_count = lax.axis_size("freq")
    count = inp_count * freq_count
    frames_all = frames_here * freq_count
    fits = (
        inputs_here == BLK
        and freq_count == 2
        and frames_here % STEP == 0
        and frames_here >= STEP + coeffs.shape[0] - 1
        and count == PLANE * PLANES
        and CH // count > LATE
        and CH // count % PAIR == 0
        and LATE % PAIR == 0
        and 2 * frames_all % LANE == 0
    )
    if not fits:
        return plain_device(voltages, coeffs)
    _, arrived, powers, *lates = front(voltages, coeffs, inp_count, freq_count, LATE)
    got = []
    for move, kept in enumerate(lates):
        pairs = [(index, moved(index, move)) for index in range(count)]
        got.append(lax.ppermute(kept, ("inp", "freq"), pairs))
    begun = correlate(arrived, powers, inp_count, freq_count, frames_all, LATE)
    if not got:
        return begun
    return correlate_late(begun, arrived, powers, got, inp_count, freq_count, frames_all, LATE)


def solution(mesh):
    in_specs = (P(("grp", "inp"), "freq", None), P())
    out_specs = P(("grp", "inp", "freq"), None, None, None, None)
    return jax.shard_map(
        per_device, mesh=mesh, in_specs=in_specs, out_specs=out_specs, check_vma=False
    )
```

```python
import functools
import math

import jax
import jax.numpy as jnp
import numpy as np
from jax import lax
from jax.experimental import pallas as pl
from jax.experimental.pallas import tpu as pltpu
from jax.sharding import PartitionSpec as P

SPF = 2048
TAPS = 8
CH = 512
CH0 = 256
INPUTS = 1024
BLK = 128


def passed_along(x, axis, by):
    length = lax.axis_size(axis)
    pairs = [(i, i + by) for i in range(length) if 0 <= i + by < length]
    return lax.ppermute(x, axis, pairs)


def make_table():
    sample = jnp.arange(SPF, dtype=jnp.int32)[:, None]
    channel = jnp.arange(CH, dtype=jnp.int32)[None, :] + CH0
    phase = sample * channel % SPF
    angle = phase.astype(jnp.float32) * (2.0 * math.pi / SPF)
    return jnp.concatenate([jnp.cos(angle), -jnp.sin(angle)], axis=1).astype(jnp.bfloat16)


def plain_device(voltages, coeffs):
    inputs_here = voltages.shape[0]
    frames_here = voltages.shape[1]
    inp_count = lax.axis_size("inp")
    freq_count = lax.axis_size("freq")
    frames_all = frames_here * freq_count
    history = voltages[:, frames_here - (TAPS - 1) :, :].astype(jnp.bfloat16)
    earlier = passed_along(history, "freq", 1)
    extended = jnp.concatenate([earlier.astype(jnp.float32), voltages.astype(jnp.float32)], axis=1)
    weights = coeffs.astype(jnp.float32)
    summed = jnp.zeros((inputs_here, frames_here, SPF), jnp.float32)
    for tap_index in range(TAPS):
        begin = TAPS - 1 - tap_index
        summed = summed + weights[tap_index] * extended[:, begin : begin + frames_here, :]
    filtered = summed.astype(jnp.bfloat16).reshape(inputs_here * frames_here, SPF)
    spectrum_t = jnp.einsum("nj,rn->jr", make_table(), filtered, preferred_element_type=jnp.float32)
    spectrum_t = spectrum_t.reshape(2 * CH, inputs_here, frames_here)
    squares = jnp.sum(spectrum_t * spectrum_t, axis=(0, 2))
    power = lax.psum(squares, "freq") / (frames_all * CH)
    gains = 1.0 / jnp.sqrt(power + 1e-06)
    scaled = (spectrum_t * gains[None, :, None]).astype(jnp.bfloat16)
    scaled = scaled.reshape(2, CH, inputs_here * frames_here)
    arrived = lax.all_to_all(scaled[None], ("inp", "freq"), split_axis=2, concat_axis=0, tiled=True)
    width_here = arrived.shape[-2]
    arranged = arrived.reshape(inp_count, freq_count, 2, width_here, inputs_here, frames_here)
    arranged = jnp.transpose(arranged, (3, 0, 4, 2, 1, 5))
    stacked = arranged.reshape(width_here, INPUTS, 2 * frames_all)
    other = jnp.concatenate([-stacked[:, :, frames_all:], stacked[:, :, :frames_all]], axis=2)
    block_count = INPUTS // BLK
    scale = 1.0 / frames_all
    pieces = []
    for row_index in range(block_count):
        row_panel = stacked[:, row_index * BLK : (row_index + 1) * BLK]
        real_part = jnp.einsum(
            "cut,cmt->cum",
            row_panel,
            stacked[:, row_index * BLK :],
            preferred_element_type=jnp.float32,
        )
        imag_part = jnp.einsum(
            "cut,cmt->cum",
            row_panel,
            other[:, row_index * BLK :],
            preferred_element_type=jnp.float32,
        )
        band = jnp.stack([real_part, imag_part], axis=1) * scale
        for col_index in range(row_index, block_count):
            begin = (col_index - row_index) * BLK
            pieces.append(band[:, :, :, begin : begin + BLK])
    return jnp.stack(pieces, axis=2).astype(jnp.bfloat16)


MESH = pl.DeviceIdType.MESH
STEP = 8
LANE = 128
PLANE = 4
PLANES = 4
LATE = 10
SIDES = 4
MOVES = 4
PAIR = 2


def table_rows(count):
    sample = np.arange(SPF, dtype=np.int32)[None, :]
    channel = np.arange(CH, dtype=np.int32)[:, None] + CH0
    angle = (sample * channel % SPF).astype(np.float32) * np.float32(2.0 * math.pi / SPF)
    both = np.stack([np.cos(angle), -np.sin(angle)])
    rows = both.reshape(2, count, CH // count, SPF).transpose(1, 0, 2, 3).reshape(2 * CH, SPF)
    return jnp.asarray(rows.astype(jnp.bfloat16))


def moved(index, move):
    plane, spot = index // PLANE, index % PLANE
    plane = (plane + PLANES // 2) % PLANES if move < 2 else PLANES - 1 - plane
    spot = spot if move % 2 == 0 else spot + 1 - 2 * (spot % 2)
    return plane * PLANE + spot


def trades_late(one, other):
    across = (one // (PLANE * 2)) != (other // (PLANE * 2))
    return across & ((one % PLANE) // 2 == (other % PLANE) // 2)


def front_kernel(inp_count, freq_count, late, *refs):
    volts, coeffs, table_hbm, spec, arrived, powers = refs[:6]
    moves = MOVES if late else 0
    lates = refs[6 : 6 + moves]
    (
        frames,
        weights,
        table,
        filtered,
        spread,
        staged,
        power,
        load_sem,
        table_sem,
        hist_send,
        hist_recv,
        stage_sem,
        send_sem,
        recv_sem,
        pow_sem,
        pow_send,
        pow_recv,
    ) = refs[6 + moves :]
    grp = lax.axis_index("grp")
    inp = lax.axis_index("inp")
    freq = lax.axis_index("freq")
    count = inp_count * freq_count
    me = inp * freq_count + freq
    inputs_here, frames_here, _ = volts.shape
    blocks = frames_here // STEP
    taps = coeffs.shape[0]
    past = taps - 1
    width = staged.shape[2]
    soon = width - late
    rows = PLANE * 2 * width
    part_cols = SPF // SIDES

    def where(index):
        return (grp, index // freq_count, index % freq_count)

    def load(t, side):
        return pltpu.make_async_copy(
            volts.at[:, t, pl.ds(side * part_cols, part_cols)],
            frames.at[t + past, :, pl.ds(side * part_cols, part_cols)],
            load_sem.at[side, t],
        )

    early = frames_here - STEP - past
    for side in range(SIDES):
        for t in range(early, frames_here):
            load(t, side).start()
    table_copy = pltpu.make_async_copy(table_hbm, table, table_sem)
    table_copy.start()

    barrier = pltpu.get_barrier_semaphore()

    def greet(step, carry):
        other = (me + step) % count
        pl.semaphore_signal(barrier, inc=1, device_id=where(other), device_id_type=MESH)
        return carry

    lax.fori_loop(1, count, greet, 0)

    def load_rest(step, carry):
        for side in range(SIDES):
            load(early - 1 - step, side).start()
        return carry

    lax.fori_loop(0, early, load_rest, 0)
    power[...] = jnp.zeros_like(power)
    weights[...] = coeffs[...].astype(jnp.float32)

    @pl.when(freq == 0)
    def _():
        def clear(step, carry):
            frames[step] = jnp.zeros((inputs_here, SPF), jnp.int32)
            return carry

        lax.fori_loop(0, past, clear, 0)

    def history_copy(step):
        return pltpu.make_async_remote_copy(
            src_ref=volts.at[:, frames_here - past + step, :],
            dst_ref=frames.at[step],
            send_sem=hist_send.at[step],
            recv_sem=hist_recv.at[step],
            device_id=(grp, inp, 1),
            device_id_type=MESH,
        )

    def filter_side(first, side):
        lanes = part_cols // LANE

        def tile(index, carry):
            row = pl.multiple_of(index // lanes * 16, 16)
            col = pl.multiple_of(side * part_cols + index % lanes * LANE, LANE)
            window = [
                frames[first + k, pl.ds(row, 16), pl.ds(col, LANE)].astype(jnp.float32)
                for k in range(STEP + past)
            ]
            scales = [
                jnp.broadcast_to(weights[k : k + 1, pl.ds(col, LANE)], (16, LANE)) for k in range(taps)
            ]
            for t in range(STEP):
                total = scales[0] * window[past + t]
                for k in range(1, taps):
                    total = total + scales[k] * window[past + t - k]
                at = pl.multiple_of(t * inputs_here + row, 16)
                filtered[pl.ds(at, 16), pl.ds(col, LANE)] = total.astype(jnp.bfloat16)
            return carry

        lax.fori_loop(0, inputs_here // 16 * lanes, tile, 0, unroll=4)

    def remote(block, other, part):
        return pltpu.make_async_remote_copy(
            src_ref=spec.at[other, block, :, pl.ds(0, part)],
            dst_ref=arrived.at[me, block, :, pl.ds(0, part)],
            send_sem=send_sem.at[block, other],
            recv_sem=recv_sem.at[block, me],
            device_id=where(other),
            device_id_type=MESH,
        )

    def landing(block, other, part):
        return pltpu.make_async_remote_copy(
            src_ref=spec.at[other, block, :, pl.ds(0, part)],
            dst_ref=arrived.at[other, block, :, pl.ds(0, part)],
            send_sem=send_sem.at[block, other],
            recv_sem=recv_sem.at[block, other],
            device_id=where(other),
            device_id_type=MESH,
        )

    def either(other, act):
        if not late:
            act(width)
            return

        @pl.when(trades_late(me, other))
        def _():
            act(soon)

        @pl.when(jnp.logical_not(trades_late(me, other)))
        def _():
            act(width)

    here = me // PLANE
    outer = (here == 0) | (here == PLANES - 1)
    near = here + 1 - 2 * (here % 2)
    jump = (here + PLANES // 2) % PLANES
    mirror = PLANES - 1 - here
    first_plane = jnp.where(outer, near, jump)
    second_plane = jnp.where(outer, jump, mirror)
    third_plane = jnp.where(outer, mirror, near)
    frames_step = STEP // 2

    def do_plane(block, plane):
        def transform(step, carry):
            lines = table[pl.ds(pl.multiple_of(plane * rows, rows), rows), :]
            at = pl.multiple_of(step * (frames_step * inputs_here), frames_step * inputs_here)
            chunk = filtered[pl.ds(at, frames_step * inputs_here), :]
            product = lax.dot_general(
                lines, chunk, (((1,), (1,)), ((), ())), preferred_element_type=jnp.float32
            )
            total = jnp.zeros((8, LANE), jnp.float32)
            for t in range(frames_step):
                piece = product[:, t * LANE : (t + 1) * LANE]
                spread[pl.ds(step * frames_step + t, rows, stride=STEP), :] = piece
                total = total + jnp.sum((piece * piece).reshape(rows // 8, 8, LANE), axis=0)
            power[...] += total
            return carry

        lax.fori_loop(0, STEP // frames_step, transform, 0)

        def convert(step, carry):
            at = pl.multiple_of(step * (2 * width * STEP), 2 * width * STEP)
            lump = spread[pl.ds(at, 2 * width * STEP), :].astype(jnp.bfloat16)
            staged[step] = lump.reshape(2, width, STEP, LANE)
            return carry

        lax.fori_loop(0, PLANE, convert, 0)

        def put_away(spot, start):
            owner = plane * PLANE + spot
            here_copy = pltpu.make_async_copy(
                staged.at[spot], arrived.at[owner, block], stage_sem.at[0, spot]
            )

            @pl.when(owner == me)
            def _():
                if start:
                    here_copy.start()
                else:
                    here_copy.wait()

            @pl.when(owner != me)
            def _():
                def act(part):
                    away = pltpu.make_async_copy(
                        staged.at[spot, :, pl.ds(0, part)],
                        spec.at[owner, block, :, pl.ds(0, part)],
                        stage_sem.at[0, spot],
                    )
                    if start:
                        away.start()
                    else:
                        away.wait()
                        remote(block, owner, part).start()

                either(owner, act)

            for move in range(moves):

                @pl.when(owner == moved(me, move))
                def _():
                    keep = pltpu.make_async_copy(
                        staged.at[spot, :, pl.ds(soon, late)], lates[move].at[block], stage_sem.at[1, spot]
                    )
                    if start:
                        keep.start()
                    else:
                        keep.wait()

        for spot in range(PLANE):
            put_away(spot, True)
        for spot in range(PLANE):
            put_away(spot, False)

    def do_block(step, carry):
        block = blocks - 1 - step
        first = block * STEP
        start = jnp.maximum(first - past, 0)
        stop = jnp.where(step == 0, frames_here, first + STEP - past)

        @pl.when((block == 0) & (freq != 0))
        def _():
            for k in range(past):
                history_copy(k).wait_recv()

        def one_side(side, inner):
            def arrive(t, innermost):
                load(t, side).wait()
                return innermost

            lax.fori_loop(start, stop, arrive, 0)
            filter_side(first, side)
            return inner

        lax.fori_loop(0, SIDES, one_side, 0)

        @pl.when(step == 0)
        def _():
            table_copy.wait()
            pl.semaphore_wait(barrier, count - 1)

            @pl.when(freq == 0)
            def _():
                for k in range(past):
                    history_copy(k).start()

        def one_plane(turn, inner):
            plane = jnp.where(
                turn == 0,
                first_plane,
                jnp.where(turn == 1, second_plane, jnp.where(turn == 2, third_plane, here)),
            )
            do_plane(block, plane)
            return inner

        lax.fori_loop(0, PLANES, one_plane, 0)
        return carry

    lax.fori_loop(0, blocks, do_block, 0)

    power_copy = pltpu.make_async_copy(power, powers.at[me], pow_sem)
    power_copy.start()
    power_copy.wait()

    def power_remote(other):
        return pltpu.make_async_remote_copy(
            src_ref=powers.at[me],
            dst_ref=powers.at[me],
            send_sem=pow_send.at[other],
            recv_sem=pow_recv.at[me],
            device_id=where(other),
            device_id_type=MESH,
        )

    def send_power(step, carry):
        power_remote((me + step) % count).start()
        return carry

    lax.fori_loop(1, count, send_power, 0)

    @pl.when(freq == 0)
    def _():
        for step in range(past):
            history_copy(step).wait_send()

    def finish(step, carry):
        other = (me + step) % count

        def act(part):
            for block in range(blocks):
                remote(block, other, part).wait_send()
                landing(block, other, part).wait_recv()

        either(other, act)
        power_remote(other).wait_send()
        pltpu.make_async_remote_copy(
            src_ref=powers.at[other],
            dst_ref=powers.at[other],
            send_sem=pow_send.at[other],
            recv_sem=pow_recv.at[other],
            device_id=where(other),
            device_id_type=MESH,
        ).wait_recv()
        return carry

    lax.fori_loop(1, count, finish, 0)


def front(voltages, coeffs, inp_count, freq_count, late):
    inputs_here, frames_here, _ = voltages.shape
    taps = coeffs.shape[0]
    count = inp_count * freq_count
    width = CH // count
    blocks = frames_here // STEP
    moves = MOVES if late else 0
    anywhere = pl.BlockSpec(memory_space=pl.ANY)
    lumps = jax.ShapeDtypeStruct((count, blocks, 2, width, STEP, LANE), jnp.bfloat16)
    kept = jax.ShapeDtypeStruct((blocks, 2, late, STEP, LANE), jnp.bfloat16)
    return pl.pallas_call(
        functools.partial(front_kernel, inp_count, freq_count, late),
        out_shape=(lumps, lumps, jax.ShapeDtypeStruct((count, 8, LANE), jnp.float32)) + (kept,) * moves,
        in_specs=[anywhere, pl.BlockSpec(memory_space=pltpu.VMEM), anywhere],
        out_specs=(anywhere,) * (3 + moves),
        scratch_shapes=[
            pltpu.VMEM((frames_here + taps - 1, inputs_here, SPF), jnp.int32),
            pltpu.VMEM((taps, SPF), jnp.float32),
            pltpu.VMEM((2 * CH, SPF), jnp.bfloat16),
            pltpu.VMEM((STEP * inputs_here, SPF), jnp.bfloat16),
            pltpu.VMEM((PLANE * 2 * width * STEP, LANE), jnp.float32),
            pltpu.VMEM((PLANE, 2, width, STEP, LANE), jnp.bfloat16),
            pltpu.VMEM((8, LANE), jnp.float32),
            pltpu.SemaphoreType.DMA((SIDES, frames_here)),
            pltpu.SemaphoreType.DMA,
            pltpu.SemaphoreType.DMA((taps - 1,)),
            pltpu.SemaphoreType.DMA((taps - 1,)),
            pltpu.SemaphoreType.DMA((2, PLANE)),
            pltpu.SemaphoreType.DMA((blocks, count)),
            pltpu.SemaphoreType.DMA((blocks, count)),
            pltpu.SemaphoreType.DMA,
            pltpu.SemaphoreType.DMA((count,)),
            pltpu.SemaphoreType.DMA((count,)),
        ],
        compiler_params=pltpu.CompilerParams(
            collective_id=0, has_side_effects=True, vmem_limit_bytes=67043328
        ),
        name="front",
    )(voltages, coeffs, table_rows(count))


def set_gains(powers, gain_row, gain_col, frames_all):
    panels = gain_row.shape[0]
    freq_count = powers.shape[0] // panels
    for panel in range(panels):
        both = powers[panel * freq_count]
        for extra in range(1, freq_count):
            both = both + powers[panel * freq_count + extra]
        power = jnp.sum(both, axis=0, keepdims=True) / (frames_all * CH)
        gain = 1.0 / jnp.sqrt(power + 1e-06)
        gain_row[panel : panel + 1, :] = gain
        wide = jnp.broadcast_to(gain * (1.0 / frames_all), (BLK, BLK))
        gain_col[panel * BLK : (panel + 1) * BLK, :] = wide.T


def correlate_channel(piece, panels, gain_row, gain_col, out, turned):
    straight, crossed = [], []
    for panel in range(panels):
        real, imag = piece(panel, 0), piece(panel, 1)
        both = jnp.concatenate([real, imag], axis=0)
        straight.append(both)
        crossed.append(jnp.concatenate([-imag, real], axis=0))
        turned[panel * BLK : (panel + 1) * BLK, :] = both.T
    for col in range(panels):
        sides = jnp.concatenate([straight[col], crossed[col]], axis=1)
        product = jnp.dot(turned[: (col + 1) * BLK, :], sides, preferred_element_type=jnp.float32)
        for row in range(col + 1):
            pair = row * panels - row * (row - 1) // 2 + col - row
            gain = gain_col[row * BLK : (row + 1) * BLK, :] * gain_row[col : col + 1, :]
            part = product[row * BLK : (row + 1) * BLK]
            out[0, pair] = (part[:, :BLK] * gain).astype(jnp.bfloat16)
            out[1, pair] = (part[:, BLK:] * gain).astype(jnp.bfloat16)


def soon_kernel(frames_all, block, powers, out, gain_row, gain_col, turned):
    panels, freq_count, blocks = block.shape[:3]

    @pl.when(pl.program_id(0) == 0)
    def _():
        set_gains(powers, gain_row, gain_col, frames_all)

    for c in range(PAIR):

        def piece(panel, side):
            parts = [block[panel, f, b, side, c] for f in range(freq_count) for b in range(blocks)]
            return jnp.concatenate(parts, axis=0)

        correlate_channel(piece, panels, gain_row, gain_col, out.at[c], turned.at[c])


def late_kernel(frames_all, freq_count, *refs):
    arrived, powers = refs[1:3]
    got = refs[3 : 3 + MOVES]
    out, held, gain_row, gain_col, turned, sem = refs[3 + MOVES :]
    count, blocks, _, late = held.shape[:4]
    panels = count // freq_count
    soon = arrived.shape[3] - late
    me = lax.axis_index("inp") * freq_count + lax.axis_index("freq")

    @pl.when(pl.program_id(0) == 0)
    def _():
        def fetch(source):
            return pltpu.make_async_copy(
                arrived.at[source, :, :, pl.ds(soon, late)], held.at[source], sem.at[source]
            )

        for source in range(count):

            @pl.when(jnp.logical_not(trades_late(me, source)))
            def _():
                fetch(source).start()

        for move in range(MOVES):
            source = moved(me, move)
            pltpu.make_async_copy(got[move], held.at[source], sem.at[source]).start()
        set_gains(powers, gain_row, gain_col, frames_all)
        for source in range(count):
            fetch(source).wait()

    for c in range(PAIR):
        at = pl.program_id(0) * PAIR + c

        def piece(panel, side):
            parts = [
                held[panel * freq_count + f, b, side, at] for f in range(freq_count) for b in range(blocks)
            ]
            return jnp.concatenate(parts, axis=0)

        correlate_channel(piece, panels, gain_row, gain_col, out.at[c], turned.at[c])


def correlate(arrived, powers, inp_count, freq_count, frames_all, late):
    count, blocks, _, width, _, _ = arrived.shape
    pairs = inp_count * (inp_count + 1) // 2
    steps = (width - late) // PAIR
    lumps = arrived.reshape(inp_count, freq_count, blocks, 2, width, STEP, LANE)
    return pl.pallas_call(
        functools.partial(soon_kernel, frames_all),
        grid=(steps,),
        out_shape=jax.ShapeDtypeStruct((width, 2, pairs, BLK, BLK), jnp.bfloat16),
        in_specs=[
            pl.BlockSpec(
                (inp_count, freq_count, blocks, 2, PAIR, STEP, LANE), lambda c: (0, 0, 0, 0, c, 0, 0)
            ),
            pl.BlockSpec((count, 8, LANE), lambda c: (0, 0, 0)),
        ],
        out_specs=pl.BlockSpec((PAIR, 2, pairs, BLK, BLK), lambda c: (c, 0, 0, 0, 0)),
        scratch_shapes=[
            pltpu.VMEM((inp_count, LANE), jnp.float32),
            pltpu.VMEM((inp_count * BLK, BLK), jnp.float32),
            pltpu.VMEM((PAIR, inp_count * BLK, 2 * frames_all), jnp.bfloat16),
        ],
        compiler_params=pltpu.CompilerParams(vmem_limit_bytes=48 * 1024 * 1024),
        cost_estimate=pl.CostEstimate(
            flops=steps * PAIR * pairs * BLK * BLK * 8 * frames_all,
            bytes_accessed=steps * PAIR * pairs * BLK * BLK * 4,
            transcendentals=0,
        ),
        name="correlate",
    )(lumps, powers)


def correlate_late(begun, arrived, powers, got, inp_count, freq_count, frames_all, late):
    count, blocks, _, width, _, _ = arrived.shape
    pairs = inp_count * (inp_count + 1) // 2
    steps, first = late // PAIR, (width - late) // PAIR
    anywhere = pl.BlockSpec(memory_space=pl.ANY)
    return pl.pallas_call(
        functools.partial(late_kernel, frames_all, freq_count),
        grid=(steps,),
        out_shape=jax.ShapeDtypeStruct(begun.shape, begun.dtype),
        in_specs=[anywhere, anywhere, pl.BlockSpec((count, 8, LANE), lambda c: (0, 0, 0))]
        + [anywhere] * MOVES,
        out_specs=pl.BlockSpec((PAIR, 2, pairs, BLK, BLK), lambda c: (first + c, 0, 0, 0, 0)),
        scratch_shapes=[
            pltpu.VMEM((count, blocks, 2, late, STEP, LANE), jnp.bfloat16),
            pltpu.VMEM((inp_count, LANE), jnp.float32),
            pltpu.VMEM((inp_count * BLK, BLK), jnp.float32),
            pltpu.VMEM((PAIR, inp_count * BLK, 2 * frames_all), jnp.bfloat16),
            pltpu.SemaphoreType.DMA((count,)),
        ],
        input_output_aliases={0: 0},
        compiler_params=pltpu.CompilerParams(vmem_limit_bytes=48 * 1024 * 1024),
        cost_estimate=pl.CostEstimate(
            flops=steps * PAIR * pairs * BLK * BLK * 8 * frames_all,
            bytes_accessed=steps * PAIR * pairs * BLK * BLK * 4,
            transcendentals=0,
        ),
        name="correlate_late",
    )(begun, arrived, powers, *got)


def per_device(voltages, coeffs):
    inputs_here, frames_here, _ = voltages.shape
    inp_count = lax.axis_size("inp")
    freq_count = lax.axis_size("freq")
    count = inp_count * freq_count
    frames_all = frames_here * freq_count
    fits = (
        inputs_here == BLK
        and freq_count == 2
        and frames_here % STEP == 0
        and frames_here >= STEP + coeffs.shape[0] - 1
        and count == PLANE * PLANES
        and CH // count > LATE
        and CH // count % PAIR == 0
        and LATE % PAIR == 0
        and 2 * frames_all % LANE == 0
    )
    if not fits:
        return plain_device(voltages, coeffs)
    _, arrived, powers, *lates = front(voltages, coeffs, inp_count, freq_count, LATE)
    got = []
    for move, kept in enumerate(lates):
        pairs = [(index, moved(index, move)) for index in range(count)]
        got.append(lax.ppermute(kept, ("inp", "freq"), pairs))
    begun = correlate(arrived, powers, inp_count, freq_count, frames_all, LATE)
    if not got:
        return begun
    return correlate_late(begun, arrived, powers, got, inp_count, freq_count, frames_all, LATE)


def solution(mesh):
    in_specs = (P(("grp", "inp"), "freq", None), P())
    out_specs = P(("grp", "inp", "freq"), None, None, None, None)
    return jax.shard_map(
        per_device, mesh=mesh, in_specs=in_specs, out_specs=out_specs, check_vma=False
    )
```

```python
import functools
import math

import jax
import jax.numpy as jnp
import numpy as np
from jax import lax
from jax.experimental import pallas as pl
from jax.experimental.pallas import tpu as pltpu
from jax.sharding import PartitionSpec as P

SPF = 2048
TAPS = 8
CH = 512
CH0 = 256
INPUTS = 1024
BLK = 128


def passed_along(x, axis, by):
    length = lax.axis_size(axis)
    pairs = [(i, i + by) for i in range(length) if 0 <= i + by < length]
    return lax.ppermute(x, axis, pairs)


def make_table():
    sample = jnp.arange(SPF, dtype=jnp.int32)[:, None]
    channel = jnp.arange(CH, dtype=jnp.int32)[None, :] + CH0
    phase = sample * channel % SPF
    angle = phase.astype(jnp.float32) * (2.0 * math.pi / SPF)
    return jnp.concatenate([jnp.cos(angle), -jnp.sin(angle)], axis=1).astype(jnp.bfloat16)


def plain_device(voltages, coeffs):
    inputs_here = voltages.shape[0]
    frames_here = voltages.shape[1]
    inp_count = lax.axis_size("inp")
    freq_count = lax.axis_size("freq")
    frames_all = frames_here * freq_count
    history = voltages[:, frames_here - (TAPS - 1) :, :].astype(jnp.bfloat16)
    earlier = passed_along(history, "freq", 1)
    extended = jnp.concatenate([earlier.astype(jnp.float32), voltages.astype(jnp.float32)], axis=1)
    weights = coeffs.astype(jnp.float32)
    summed = jnp.zeros((inputs_here, frames_here, SPF), jnp.float32)
    for tap_index in range(TAPS):
        begin = TAPS - 1 - tap_index
        summed = summed + weights[tap_index] * extended[:, begin : begin + frames_here, :]
    filtered = summed.astype(jnp.bfloat16).reshape(inputs_here * frames_here, SPF)
    spectrum_t = jnp.einsum("nj,rn->jr", make_table(), filtered, preferred_element_type=jnp.float32)
    spectrum_t = spectrum_t.reshape(2 * CH, inputs_here, frames_here)
    squares = jnp.sum(spectrum_t * spectrum_t, axis=(0, 2))
    power = lax.psum(squares, "freq") / (frames_all * CH)
    gains = 1.0 / jnp.sqrt(power + 1e-06)
    scaled = (spectrum_t * gains[None, :, None]).astype(jnp.bfloat16)
    scaled = scaled.reshape(2, CH, inputs_here * frames_here)
    arrived = lax.all_to_all(scaled[None], ("inp", "freq"), split_axis=2, concat_axis=0, tiled=True)
    width_here = arrived.shape[-2]
    arranged = arrived.reshape(inp_count, freq_count, 2, width_here, inputs_here, frames_here)
    arranged = jnp.transpose(arranged, (3, 0, 4, 2, 1, 5))
    stacked = arranged.reshape(width_here, INPUTS, 2 * frames_all)
    other = jnp.concatenate([-stacked[:, :, frames_all:], stacked[:, :, :frames_all]], axis=2)
    block_count = INPUTS // BLK
    scale = 1.0 / frames_all
    pieces = []
    for row_index in range(block_count):
        row_panel = stacked[:, row_index * BLK : (row_index + 1) * BLK]
        real_part = jnp.einsum(
            "cut,cmt->cum",
            row_panel,
            stacked[:, row_index * BLK :],
            preferred_element_type=jnp.float32,
        )
        imag_part = jnp.einsum(
            "cut,cmt->cum",
            row_panel,
            other[:, row_index * BLK :],
            preferred_element_type=jnp.float32,
        )
        band = jnp.stack([real_part, imag_part], axis=1) * scale
        for col_index in range(row_index, block_count):
            begin = (col_index - row_index) * BLK
            pieces.append(band[:, :, :, begin : begin + BLK])
    return jnp.stack(pieces, axis=2).astype(jnp.bfloat16)


MESH = pl.DeviceIdType.MESH
STEP = 8
LANE = 128
PLANE = 4
PLANES = 4
LATE = 10
SIDES = 4
MOVES = 4
PAIR = 2


def table_rows(count):
    sample = np.arange(SPF // 2, dtype=np.int32)[None, :]
    channel = np.arange(CH, dtype=np.int32)[:, None] + CH0
    angle = (sample * channel % SPF).astype(np.float32) * np.float32(2.0 * math.pi / SPF)
    both = np.stack([np.cos(angle), -np.sin(angle)])
    rows = both.reshape(2, count, CH // count, SPF // 2).transpose(1, 0, 2, 3).reshape(2 * CH, SPF // 2)
    return jnp.asarray(rows.astype(jnp.bfloat16))


def moved(index, move):
    plane, spot = index // PLANE, index % PLANE
    plane = (plane + PLANES // 2) % PLANES if move < 2 else PLANES - 1 - plane
    spot = spot if move % 2 == 0 else spot + 1 - 2 * (spot % 2)
    return plane * PLANE + spot


def trades_late(one, other):
    across = (one // (PLANE * 2)) != (other // (PLANE * 2))
    return across & ((one % PLANE) // 2 == (other % PLANE) // 2)


def front_kernel(inp_count, freq_count, late, *refs):
    volts, coeffs, table_hbm, spec, arrived, powers = refs[:6]
    moves = MOVES if late else 0
    lates = refs[6 : 6 + moves]
    (
        frames,
        weights,
        table,
        filtered,
        spread,
        staged,
        power,
        load_sem,
        table_sem,
        hist_send,
        hist_recv,
        stage_sem,
        send_sem,
        recv_sem,
        pow_sem,
        pow_send,
        pow_recv,
    ) = refs[6 + moves :]
    grp = lax.axis_index("grp")
    inp = lax.axis_index("inp")
    freq = lax.axis_index("freq")
    count = inp_count * freq_count
    me = inp * freq_count + freq
    inputs_here, frames_here, _ = volts.shape
    blocks = frames_here // STEP
    taps = coeffs.shape[0]
    past = taps - 1
    width = staged.shape[2]
    soon = width - late
    rows = PLANE * 2 * width
    part_cols = SPF // SIDES

    def where(index):
        return (grp, index // freq_count, index % freq_count)

    def load(t, side):
        return pltpu.make_async_copy(
            volts.at[:, t, pl.ds(side * part_cols, part_cols)],
            frames.at[t + past, :, pl.ds(side * part_cols, part_cols)],
            load_sem.at[side, t],
        )

    early = frames_here - STEP - past
    for side in range(SIDES):
        for t in range(early, frames_here):
            load(t, side).start()
    table_copy = pltpu.make_async_copy(table_hbm, table.at[:, pl.ds(0, SPF // 2)], table_sem)
    table_copy.start()

    barrier = pltpu.get_barrier_semaphore()

    def greet(step, carry):
        other = (me + step) % count
        pl.semaphore_signal(barrier, inc=1, device_id=where(other), device_id_type=MESH)
        return carry

    lax.fori_loop(1, count, greet, 0)

    def load_rest(step, carry):
        for side in range(SIDES):
            load(early - 1 - step, side).start()
        return carry

    lax.fori_loop(0, early, load_rest, 0)
    power[...] = jnp.zeros_like(power)
    weights[...] = coeffs[...].astype(jnp.float32)

    @pl.when(freq == 0)
    def _():
        def clear(step, carry):
            frames[step] = jnp.zeros((inputs_here, SPF), jnp.int32)
            return carry

        lax.fori_loop(0, past, clear, 0)

    def history_copy(step):
        return pltpu.make_async_remote_copy(
            src_ref=volts.at[:, frames_here - past + step, :],
            dst_ref=frames.at[step],
            send_sem=hist_send.at[step],
            recv_sem=hist_recv.at[step],
            device_id=(grp, inp, 1),
            device_id_type=MESH,
        )

    def filter_side(first, side):
        lanes = part_cols // LANE

        def tile(index, carry):
            row = pl.multiple_of(index // lanes * 16, 16)
            col = pl.multiple_of(side * part_cols + index % lanes * LANE, LANE)
            window = [
                frames[first + k, pl.ds(row, 16), pl.ds(col, LANE)].astype(jnp.float32)
                for k in range(STEP + past)
            ]
            scales = [
                jnp.broadcast_to(weights[k : k + 1, pl.ds(col, LANE)], (16, LANE)) for k in range(taps)
            ]
            for t in range(STEP):
                total = scales[0] * window[past + t]
                for k in range(1, taps):
                    total = total + scales[k] * window[past + t - k]
                at = pl.multiple_of(t * inputs_here + row, 16)
                filtered[pl.ds(at, 16), pl.ds(col, LANE)] = total.astype(jnp.bfloat16)
            return carry

        lax.fori_loop(0, inputs_here // 16 * lanes, tile, 0, unroll=4)

    def remote(block, other, part):
        return pltpu.make_async_remote_copy(
            src_ref=spec.at[other, block, :, pl.ds(0, part)],
            dst_ref=arrived.at[me, block, :, pl.ds(0, part)],
            send_sem=send_sem.at[block, other],
            recv_sem=recv_sem.at[block, me],
            device_id=where(other),
            device_id_type=MESH,
        )

    def landing(block, other, part):
        return pltpu.make_async_remote_copy(
            src_ref=spec.at[other, block, :, pl.ds(0, part)],
            dst_ref=arrived.at[other, block, :, pl.ds(0, part)],
            send_sem=send_sem.at[block, other],
            recv_sem=recv_sem.at[block, other],
            device_id=where(other),
            device_id_type=MESH,
        )

    def either(other, act):
        if not late:
            act(width)
            return

        @pl.when(trades_late(me, other))
        def _():
            act(soon)

        @pl.when(jnp.logical_not(trades_late(me, other)))
        def _():
            act(width)

    here = me // PLANE
    outer = (here == 0) | (here == PLANES - 1)
    near = here + 1 - 2 * (here % 2)
    jump = (here + PLANES // 2) % PLANES
    mirror = PLANES - 1 - here
    first_plane = jnp.where(outer, near, jump)
    second_plane = jnp.where(outer, jump, mirror)
    third_plane = jnp.where(outer, mirror, near)
    frames_step = STEP // 2

    def do_plane(block, plane):
        def transform(step, carry):
            lines = table[pl.ds(pl.multiple_of(plane * rows, rows), rows), :]
            at = pl.multiple_of(step * (frames_step * inputs_here), frames_step * inputs_here)
            chunk = filtered[pl.ds(at, frames_step * inputs_here), :]
            product = lax.dot_general(
                lines, chunk, (((1,), (1,)), ((), ())), preferred_element_type=jnp.float32
            )
            total = jnp.zeros((8, LANE), jnp.float32)
            for t in range(frames_step):
                piece = product[:, t * LANE : (t + 1) * LANE]
                spread[pl.ds(step * frames_step + t, rows, stride=STEP), :] = piece
                total = total + jnp.sum((piece * piece).reshape(rows // 8, 8, LANE), axis=0)
            power[...] += total
            return carry

        lax.fori_loop(0, STEP // frames_step, transform, 0)

        def convert(step, carry):
            at = pl.multiple_of(step * (2 * width * STEP), 2 * width * STEP)
            lump = spread[pl.ds(at, 2 * width * STEP), :].astype(jnp.bfloat16)
            staged[step] = lump.reshape(2, width, STEP, LANE)
            return carry

        lax.fori_loop(0, PLANE, convert, 0)

        def put_away(spot, start):
            owner = plane * PLANE + spot
            here_copy = pltpu.make_async_copy(
                staged.at[spot], arrived.at[owner, block], stage_sem.at[0, spot]
            )

            @pl.when(owner == me)
            def _():
                if start:
                    here_copy.start()
                else:
                    here_copy.wait()

            @pl.when(owner != me)
            def _():
                def act(part):
                    away = pltpu.make_async_copy(
                        staged.at[spot, :, pl.ds(0, part)],
                        spec.at[owner, block, :, pl.ds(0, part)],
                        stage_sem.at[0, spot],
                    )
                    if start:
                        away.start()
                    else:
                        away.wait()
                        remote(block, owner, part).start()

                either(owner, act)

            for move in range(moves):

                @pl.when(owner == moved(me, move))
                def _():
                    keep = pltpu.make_async_copy(
                        staged.at[spot, :, pl.ds(soon, late)], lates[move].at[block], stage_sem.at[1, spot]
                    )
                    if start:
                        keep.start()
                    else:
                        keep.wait()

        for spot in range(PLANE):
            put_away(spot, True)
        for spot in range(PLANE):
            put_away(spot, False)

    def do_block(step, carry):
        block = blocks - 1 - step
        first = block * STEP
        start = jnp.maximum(first - past, 0)
        stop = jnp.where(step == 0, frames_here, first + STEP - past)

        @pl.when((block == 0) & (freq != 0))
        def _():
            for k in range(past):
                history_copy(k).wait_recv()

        def one_side(side, inner):
            def arrive(t, innermost):
                load(t, side).wait()
                return innermost

            lax.fori_loop(start, stop, arrive, 0)
            filter_side(first, side)
            return inner

        lax.fori_loop(0, SIDES, one_side, 0)

        @pl.when(step == 0)
        def _():
            table_copy.wait()
            odd = lax.broadcasted_iota(jnp.int32, (16, LANE), 0) % 2
            sign = (1 - 2 * odd).astype(jnp.float32).astype(jnp.bfloat16)

            def extend(turn, innermost):
                at = pl.multiple_of(turn * 16, 16)
                for col in range(0, SPF // 2, LANE):
                    first_half = table[pl.ds(at, 16), col : col + LANE]
                    table[pl.ds(at, 16), SPF // 2 + col : SPF // 2 + col + LANE] = first_half * sign
                return innermost

            lax.fori_loop(0, 2 * CH // 16, extend, 0)
            pl.semaphore_wait(barrier, count - 1)

            @pl.when(freq == 0)
            def _():
                for k in range(past):
                    history_copy(k).start()

        def one_plane(turn, inner):
            plane = jnp.where(
                turn == 0,
                first_plane,
                jnp.where(turn == 1, second_plane, jnp.where(turn == 2, third_plane, here)),
            )
            do_plane(block, plane)
            return inner

        lax.fori_loop(0, PLANES, one_plane, 0)
        return carry

    lax.fori_loop(0, blocks, do_block, 0)

    power_copy = pltpu.make_async_copy(power, powers.at[me], pow_sem)
    power_copy.start()
    power_copy.wait()

    def power_remote(other):
        return pltpu.make_async_remote_copy(
            src_ref=powers.at[me],
            dst_ref=powers.at[me],
            send_sem=pow_send.at[other],
            recv_sem=pow_recv.at[me],
            device_id=where(other),
            device_id_type=MESH,
        )

    def send_power(step, carry):
        power_remote((me + step) % count).start()
        return carry

    lax.fori_loop(1, count, send_power, 0)

    @pl.when(freq == 0)
    def _():
        for step in range(past):
            history_copy(step).wait_send()

    def finish(step, carry):
        other = (me + step) % count

        def act(part):
            for block in range(blocks):
                remote(block, other, part).wait_send()
                landing(block, other, part).wait_recv()

        either(other, act)
        power_remote(other).wait_send()
        pltpu.make_async_remote_copy(
            src_ref=powers.at[other],
            dst_ref=powers.at[other],
            send_sem=pow_send.at[other],
            recv_sem=pow_recv.at[other],
            device_id=where(other),
            device_id_type=MESH,
        ).wait_recv()
        return carry

    lax.fori_loop(1, count, finish, 0)


def front(voltages, coeffs, inp_count, freq_count, late):
    inputs_here, frames_here, _ = voltages.shape
    taps = coeffs.shape[0]
    count = inp_count * freq_count
    width = CH // count
    blocks = frames_here // STEP
    moves = MOVES if late else 0
    anywhere = pl.BlockSpec(memory_space=pl.ANY)
    lumps = jax.ShapeDtypeStruct((count, blocks, 2, width, STEP, LANE), jnp.bfloat16)
    kept = jax.ShapeDtypeStruct((blocks, 2, late, STEP, LANE), jnp.bfloat16)
    return pl.pallas_call(
        functools.partial(front_kernel, inp_count, freq_count, late),
        out_shape=(lumps, lumps, jax.ShapeDtypeStruct((count, 8, LANE), jnp.float32)) + (kept,) * moves,
        in_specs=[anywhere, pl.BlockSpec(memory_space=pltpu.VMEM), anywhere],
        out_specs=(anywhere,) * (3 + moves),
        scratch_shapes=[
            pltpu.VMEM((frames_here + taps - 1, inputs_here, SPF), jnp.int32),
            pltpu.VMEM((taps, SPF), jnp.float32),
            pltpu.VMEM((2 * CH, SPF), jnp.bfloat16),
            pltpu.VMEM((STEP * inputs_here, SPF), jnp.bfloat16),
            pltpu.VMEM((PLANE * 2 * width * STEP, LANE), jnp.float32),
            pltpu.VMEM((PLANE, 2, width, STEP, LANE), jnp.bfloat16),
            pltpu.VMEM((8, LANE), jnp.float32),
            pltpu.SemaphoreType.DMA((SIDES, frames_here)),
            pltpu.SemaphoreType.DMA,
            pltpu.SemaphoreType.DMA((taps - 1,)),
            pltpu.SemaphoreType.DMA((taps - 1,)),
            pltpu.SemaphoreType.DMA((2, PLANE)),
            pltpu.SemaphoreType.DMA((blocks, count)),
            pltpu.SemaphoreType.DMA((blocks, count)),
            pltpu.SemaphoreType.DMA,
            pltpu.SemaphoreType.DMA((count,)),
            pltpu.SemaphoreType.DMA((count,)),
        ],
        compiler_params=pltpu.CompilerParams(
            collective_id=0, has_side_effects=True, vmem_limit_bytes=67043328
        ),
        name="front",
    )(voltages, coeffs, table_rows(count))


def set_gains(powers, gain_row, gain_col, frames_all):
    panels = gain_row.shape[0]
    freq_count = powers.shape[0] // panels
    for panel in range(panels):
        both = powers[panel * freq_count]
        for extra in range(1, freq_count):
            both = both + powers[panel * freq_count + extra]
        power = jnp.sum(both, axis=0, keepdims=True) / (frames_all * CH)
        gain = 1.0 / jnp.sqrt(power + 1e-06)
        gain_row[panel : panel + 1, :] = gain
        wide = jnp.broadcast_to(gain * (1.0 / frames_all), (BLK, BLK))
        gain_col[panel * BLK : (panel + 1) * BLK, :] = wide.T


def correlate_channel(piece, panels, gain_row, gain_col, out, turned):
    straight, crossed = [], []
    for panel in range(panels):
        real, imag = piece(panel, 0), piece(panel, 1)
        both = jnp.concatenate([real, imag], axis=0)
        straight.append(both)
        crossed.append(jnp.concatenate([-imag, real], axis=0))
        turned[panel * BLK : (panel + 1) * BLK, :] = both.T
    for col in range(panels):
        sides = jnp.concatenate([straight[col], crossed[col]], axis=1)
        product = jnp.dot(turned[: (col + 1) * BLK, :], sides, preferred_element_type=jnp.float32)
        for row in range(col + 1):
            pair = row * panels - row * (row - 1) // 2 + col - row
            gain = gain_col[row * BLK : (row + 1) * BLK, :] * gain_row[col : col + 1, :]
            part = product[row * BLK : (row + 1) * BLK]
            out[0, pair] = (part[:, :BLK] * gain).astype(jnp.bfloat16)
            out[1, pair] = (part[:, BLK:] * gain).astype(jnp.bfloat16)


def soon_kernel(frames_all, block, powers, out, gain_row, gain_col, turned):
    panels, freq_count, blocks = block.shape[:3]

    @pl.when(pl.program_id(0) == 0)
    def _():
        set_gains(powers, gain_row, gain_col, frames_all)

    for c in range(PAIR):

        def piece(panel, side):
            parts = [block[panel, f, b, side, c] for f in range(freq_count) for b in range(blocks)]
            return jnp.concatenate(parts, axis=0)

        correlate_channel(piece, panels, gain_row, gain_col, out.at[c], turned.at[c])


def late_kernel(frames_all, freq_count, *refs):
    arrived, powers = refs[1:3]
    got = refs[3 : 3 + MOVES]
    out, held, gain_row, gain_col, turned, sem = refs[3 + MOVES :]
    count, blocks, _, late = held.shape[:4]
    panels = count // freq_count
    soon = arrived.shape[3] - late
    me = lax.axis_index("inp") * freq_count + lax.axis_index("freq")

    def fetch(source, pair):
        return pltpu.make_async_copy(
            arrived.at[source, :, :, pl.ds(soon + pair * PAIR, PAIR)],
            held.at[source, :, :, pl.ds(pair * PAIR, PAIR)],
            sem.at[source, pair],
        )

    @pl.when(pl.program_id(0) == 0)
    def _():
        for pair in range(late // PAIR):
            for move in range(MOVES):
                source = moved(me, move)
                pltpu.make_async_copy(
                    got[move].at[:, :, pl.ds(pair * PAIR, PAIR)],
                    held.at[source, :, :, pl.ds(pair * PAIR, PAIR)],
                    sem.at[source, pair],
                ).start()
            for source in range(count):

                @pl.when(jnp.logical_not(trades_late(me, source)))
                def _():
                    fetch(source, pair).start()

        set_gains(powers, gain_row, gain_col, frames_all)

    for source in range(count):
        fetch(source, pl.program_id(0)).wait()

    for c in range(PAIR):
        at = pl.program_id(0) * PAIR + c

        def piece(panel, side):
            parts = [
                held[panel * freq_count + f, b, side, at] for f in range(freq_count) for b in range(blocks)
            ]
            return jnp.concatenate(parts, axis=0)

        correlate_channel(piece, panels, gain_row, gain_col, out.at[c], turned.at[c])


def correlate(arrived, powers, inp_count, freq_count, frames_all, late):
    count, blocks, _, width, _, _ = arrived.shape
    pairs = inp_count * (inp_count + 1) // 2
    steps = (width - late) // PAIR
    lumps = arrived.reshape(inp_count, freq_count, blocks, 2, width, STEP, LANE)
    return pl.pallas_call(
        functools.partial(soon_kernel, frames_all),
        grid=(steps,),
        out_shape=jax.ShapeDtypeStruct((width, 2, pairs, BLK, BLK), jnp.bfloat16),
        in_specs=[
            pl.BlockSpec(
                (inp_count, freq_count, blocks, 2, PAIR, STEP, LANE), lambda c: (0, 0, 0, 0, c, 0, 0)
            ),
            pl.BlockSpec((count, 8, LANE), lambda c: (0, 0, 0)),
        ],
        out_specs=pl.BlockSpec((PAIR, 2, pairs, BLK, BLK), lambda c: (c, 0, 0, 0, 0)),
        scratch_shapes=[
            pltpu.VMEM((inp_count, LANE), jnp.float32),
            pltpu.VMEM((inp_count * BLK, BLK), jnp.float32),
            pltpu.VMEM((PAIR, inp_count * BLK, 2 * frames_all), jnp.bfloat16),
        ],
        compiler_params=pltpu.CompilerParams(vmem_limit_bytes=48 * 1024 * 1024),
        cost_estimate=pl.CostEstimate(
            flops=steps * PAIR * pairs * BLK * BLK * 8 * frames_all,
            bytes_accessed=steps * PAIR * pairs * BLK * BLK * 4,
            transcendentals=0,
        ),
        name="correlate",
    )(lumps, powers)


def correlate_late(begun, arrived, powers, got, inp_count, freq_count, frames_all, late):
    count, blocks, _, width, _, _ = arrived.shape
    pairs = inp_count * (inp_count + 1) // 2
    steps, first = late // PAIR, (width - late) // PAIR
    anywhere = pl.BlockSpec(memory_space=pl.ANY)
    return pl.pallas_call(
        functools.partial(late_kernel, frames_all, freq_count),
        grid=(steps,),
        out_shape=jax.ShapeDtypeStruct(begun.shape, begun.dtype),
        in_specs=[anywhere, anywhere, pl.BlockSpec((count, 8, LANE), lambda c: (0, 0, 0))]
        + [anywhere] * MOVES,
        out_specs=pl.BlockSpec((PAIR, 2, pairs, BLK, BLK), lambda c: (first + c, 0, 0, 0, 0)),
        scratch_shapes=[
            pltpu.VMEM((count, blocks, 2, late, STEP, LANE), jnp.bfloat16),
            pltpu.VMEM((inp_count, LANE), jnp.float32),
            pltpu.VMEM((inp_count * BLK, BLK), jnp.float32),
            pltpu.VMEM((PAIR, inp_count * BLK, 2 * frames_all), jnp.bfloat16),
            pltpu.SemaphoreType.DMA((count, steps)),
        ],
        input_output_aliases={0: 0},
        compiler_params=pltpu.CompilerParams(vmem_limit_bytes=48 * 1024 * 1024),
        cost_estimate=pl.CostEstimate(
            flops=steps * PAIR * pairs * BLK * BLK * 8 * frames_all,
            bytes_accessed=steps * PAIR * pairs * BLK * BLK * 4,
            transcendentals=0,
        ),
        name="correlate_late",
    )(begun, arrived, powers, *got)


def per_device(voltages, coeffs):
    inputs_here, frames_here, _ = voltages.shape
    inp_count = lax.axis_size("inp")
    freq_count = lax.axis_size("freq")
    count = inp_count * freq_count
    frames_all = frames_here * freq_count
    fits = (
        inputs_here == BLK
        and freq_count == 2
        and frames_here % STEP == 0
        and frames_here >= STEP + coeffs.shape[0] - 1
        and count == PLANE * PLANES
        and CH // count > LATE
        and CH // count % PAIR == 0
        and LATE % PAIR == 0
        and CH0 % 2 == 0
        and 2 * frames_all % LANE == 0
    )
    if not fits:
        return plain_device(voltages, coeffs)
    _, arrived, powers, *lates = front(voltages, coeffs, inp_count, freq_count, LATE)
    got = []
    for move, kept in enumerate(lates):
        pairs = [(index, moved(index, move)) for index in range(count)]
        got.append(lax.ppermute(kept, ("inp", "freq"), pairs))
    begun = correlate(arrived, powers, inp_count, freq_count, frames_all, LATE)
    if not got:
        return begun
    return correlate_late(begun, arrived, powers, got, inp_count, freq_count, frames_all, LATE)


def solution(mesh):
    in_specs = (P(("grp", "inp"), "freq", None), P())
    out_specs = P(("grp", "inp", "freq"), None, None, None, None)
    return jax.shard_map(
        per_device, mesh=mesh, in_specs=in_specs, out_specs=out_specs, check_vma=False
    )
```
